32 devices in a mesh: seq: 8 (over z, x), fsdp: 4 (over y, core).
Axes of the slice: x: 2, y: 2, z: 4, core: 2. Of those that a mesh axis runs over, the one named last changes fastest.
Arguments:
- hidden_in: bfloat16 [4, 2048, 1024], P('fsdp', 'seq'), may hold values from -6 to 6
- w_qkv: bfloat16 [1024, 1536], P('fsdp'), may hold values from -1 to 1
- w_out: bfloat16 [512, 1024], P('fsdp'), may hold values from -0.75 to 0.75
- w_in: bfloat16 [1024, 2624], P('fsdp'), may hold values from -0.1875 to 0.1875
- w_down: bfloat16 [1312, 1024], P('fsdp'), may hold values from -0.15625 to 0.15625
- norm_scales: float32 [2, 1024], P(None, 'fsdp'), may hold values from 0.5 to 1.5
- cotangent: bfloat16 [4, 2048, 1024], P('fsdp', 'seq'), may hold values from -6 to 6
Outputs:
- layer_out: bfloat16 [4, 2048, 1024], P('fsdp', 'seq')
- grad_input: float32 [4, 2048, 1024], P('fsdp', 'seq')
- grad_w_qkv: float32 [1024, 1536], P('fsdp')
- grad_w_out: float32 [512, 1024], P('fsdp')
- grad_w_in: float32 [1024, 2624], P('fsdp')
- grad_w_down: float32 [1312, 1024], P('fsdp')
- grad_scales: float32 [2, 1024], P(None, 'fsdp')
The draws below stay inside these ranges and needn't reach their ends.
All inputs are finite; a program needn't handle non-finite values.
Results may differ from the reference program's by a relative error of at most 0.033.
Values may be sent and summed in bfloat16 or wider, within the bound.
No kernel may reach another device: no remote copies, remote signals or barrier semaphores. Data moves between devices by JAX's collectives and lax.ppermute only.
A program may use at most 128 MiB of HBM per device.

```python
import math
import jax
import jax.numpy as jnp
from jax import lax

D = 1024
HEADS = 8
HEAD = 64
FF = 1312
WIN = 64
BATCH = 4
LENGTH = 2048


def draw_w_qkv(key, part):
    inner_dim = HEADS * HEAD
    base_key = jax.random.fold_in(jax.random.fold_in(key, 11), 0)
    jitter_key = jax.random.fold_in(jax.random.fold_in(key, 11), 1)
    value_key = jax.random.fold_in(jax.random.fold_in(key, 11), 3)
    query_cols = jax.random.normal(base_key, (D, inner_dim), jnp.float32)
    key_cols = jax.random.normal(jitter_key, (D, inner_dim), jnp.float32)
    value_cols = jax.random.normal(value_key, (D, inner_dim), jnp.float32)
    stacked = jnp.concatenate([query_cols, key_cols, value_cols], axis=1) * (1.0 / math.sqrt(D))
    return jnp.clip(stacked, -1.0, 1.0).astype(jnp.bfloat16)


def shard_levels(own_key, extent, pieces, least, top_value):
    level = 1.0
    for position, shards_of in pieces:
        draws = jax.random.uniform(jax.random.fold_in(jax.random.fold_in(own_key, 6), position), (shards_of,), jnp.float32, least / len(pieces), top_value / len(pieces))
        level = level * jnp.repeat(jnp.exp(draws), extent[position] // shards_of).reshape((-1,) + (1,) * (len(extent) - 1 - position))
    return level


def gaussian(stream_key, extent, width, most, shards=(), kind=jnp.bfloat16):
    values = width * jax.random.normal(stream_key, extent, jnp.float32)
    if shards:
        values = values * shard_levels(stream_key, extent, shards, -0.22, 0.18)
    return jnp.clip(values, -most, most).astype(kind)


def setup_inputs(seed: int = 0) -> dict:
    streams_of = jax.random.split(jax.random.key(seed), 8)
    hidden_in = gaussian(streams_of[0], (BATCH, LENGTH, D), 1.0, 6.0, ((0, 4), (1, 8)))
    w_qkv = draw_w_qkv(jax.random.fold_in(streams_of[7], 71), 0)
    w_out = gaussian(streams_of[2], (HEADS * HEAD, D), (max(HEADS * HEAD // 8, 1)) ** -0.5, 0.75, ((0, 4),))
    w_in = gaussian(streams_of[3], (D, 2 * FF), D ** -0.5, 0.1875, ((0, 4),))
    w_down = gaussian(streams_of[4], (FF, D), FF ** -0.5, 0.15625, ((0, 4),))
    norm_scales = jnp.clip(1.0 + 0.1 * jax.random.normal(streams_of[5], (2, D), jnp.float32), 0.5, 1.5)
    cotangent = gaussian(streams_of[6], (BATCH, LENGTH, D), 1.0, 6.0, ((0, 4), (1, 8)))
    return dict(hidden_in=hidden_in, w_qkv=w_qkv, w_out=w_out, w_in=w_in, w_down=w_down, norm_scales=norm_scales, cotangent=cotangent)


norm_eps = 1e-05
rope_theta = 10000.0

def rounded(values):
    return lax.optimization_barrier(values.astype(jnp.bfloat16))

def layer_norm(residual, gain_vec):
    average = lax.optimization_barrier(jnp.mean(residual, axis=-1, keepdims=True))
    centred = residual - average
    variance = lax.optimization_barrier(jnp.mean(centred * centred, axis=-1, keepdims=True))
    inv_std = lax.rsqrt(variance + norm_eps)
    normed = centred * inv_std
    return (normed, inv_std, normed * gain_vec)

def norm_back(upstream, normed, inv_std, gain_vec):
    through = upstream * gain_vec
    first_mean = lax.optimization_barrier(jnp.mean(through, axis=-1, keepdims=True))
    second_mean = lax.optimization_barrier(jnp.mean(through * normed, axis=-1, keepdims=True))
    return inv_std * (through - first_mean - normed * second_mean)

def rope_tables(positions):
    half_dim = HEAD // 2
    frequency = jnp.exp(jnp.arange(half_dim, dtype=jnp.float32) * (-2.0 * math.log(rope_theta) / HEAD))
    angles = positions.astype(jnp.float32)[:, None] * frequency[None, :]
    angles = jnp.concatenate([angles, angles], axis=1)
    return (jnp.cos(angles)[:, None, :], jnp.sin(angles)[:, None, :])

def rotate_half(values):
    half_dim = values.shape[-1] // 2
    return jnp.concatenate([-values[..., half_dim:], values[..., :half_dim]], axis=-1)

def band_mask(offset, query_count, key_count, length_all):
    query_pos = offset + jnp.arange(query_count, dtype=jnp.int32)[:, None]
    key_pos = offset - WIN + jnp.arange(key_count, dtype=jnp.int32)[None, :]
    in_window = jnp.abs(query_pos - key_pos) <= WIN
    return in_window & (key_pos >= 0) & (key_pos < length_all)

def gelu_parts(act_in):
    cumulative = 0.5 * (1.0 + lax.erf(act_in * (1.0 / math.sqrt(2.0))))
    density = jnp.exp(-0.5 * act_in * act_in) * (1.0 / math.sqrt(2.0 * math.pi))
    return (act_in * cumulative, cumulative + act_in * density)

def attend_forward(query_rot, key_rot, value_b, block_rows):
    length_all = query_rot.shape[0]
    pad_spec = ((WIN, WIN), (0, 0), (0, 0))
    key_pad = jnp.pad(key_rot, pad_spec)
    value_pad = jnp.pad(value_b, pad_spec)
    score_scale = 1.0 / math.sqrt(HEAD)

    def one_block(block_idx):
        offset = block_idx * block_rows
        query_blk = lax.dynamic_slice_in_dim(query_rot, offset, block_rows, 0).astype(jnp.float32)
        key_blk = lax.dynamic_slice_in_dim(key_pad, offset, block_rows + 2 * WIN, 0).astype(jnp.float32)
        value_blk = lax.dynamic_slice_in_dim(value_pad, offset, block_rows + 2 * WIN, 0).astype(jnp.float32)
        scores = jnp.einsum('qhe,khe->hqk', query_blk, key_blk) * score_scale
        allowed = band_mask(offset, block_rows, block_rows + 2 * WIN, length_all)
        scores = jnp.where(allowed[None], scores, -jnp.inf)
        top_score = lax.optimization_barrier(jnp.max(scores, axis=-1, keepdims=True))
        totals = lax.optimization_barrier(jnp.sum(jnp.exp(scores - top_score), axis=-1, keepdims=True))
        log_total = top_score + jnp.log(totals)
        probs_b = rounded(jnp.exp(scores - log_total))
        context = jnp.einsum('hqk,khe->qhe', probs_b.astype(jnp.float32), value_blk)
        return (rounded(context), log_total[..., 0])
    context, log_total = lax.map(one_block, jnp.arange(length_all // block_rows, dtype=jnp.int32))
    return (context.reshape(length_all, HEADS * HEAD), log_total)

def attend_backward(query_rot, key_rot, value_b, context, log_total, grad_context, block_rows):
    length_all = query_rot.shape[0]
    pad_spec = ((WIN, WIN), (0, 0), (0, 0))
    key_pad = jnp.pad(key_rot, pad_spec)
    value_pad = jnp.pad(value_b, pad_spec)
    score_scale = 1.0 / math.sqrt(HEAD)
    context_heads = context.reshape(length_all, HEADS, HEAD).astype(jnp.float32)
    grad_heads = grad_context.reshape(length_all, HEADS, HEAD).astype(jnp.float32)
    delta_all = lax.optimization_barrier(jnp.sum(grad_heads * context_heads, axis=-1))
    zero_pad = jnp.zeros((length_all + 2 * WIN, HEADS, HEAD), jnp.float32)

    def one_block(running, block_idx):
        key_acc, value_acc = running
        offset = block_idx * block_rows
        span = block_rows + 2 * WIN
        query_blk = lax.dynamic_slice_in_dim(query_rot, offset, block_rows, 0).astype(jnp.float32)
        key_blk = lax.dynamic_slice_in_dim(key_pad, offset, span, 0).astype(jnp.float32)
        value_blk = lax.dynamic_slice_in_dim(value_pad, offset, span, 0).astype(jnp.float32)
        grad_blk = lax.dynamic_slice_in_dim(grad_heads, offset, block_rows, 0)
        delta_blk = lax.dynamic_slice_in_dim(delta_all, offset, block_rows, 0)
        log_blk = log_total[block_idx]
        scores = jnp.einsum('qhe,khe->hqk', query_blk, key_blk) * score_scale
        allowed = band_mask(offset, block_rows, span, length_all)
        scores = jnp.where(allowed[None], scores, -jnp.inf)
        probs_f = jnp.exp(scores - log_blk[..., None])
        probs_b = rounded(probs_f).astype(jnp.float32)
        grad_value = jnp.einsum('hqk,qhe->khe', probs_b, grad_blk)
        grad_probs = jnp.einsum('qhe,khe->hqk', grad_blk, value_blk)
        grad_scores = rounded(probs_f * (grad_probs - delta_blk.T[:, :, None]) * score_scale).astype(jnp.float32)
        grad_query = jnp.einsum('hqk,khe->qhe', grad_scores, key_blk)
        grad_key = jnp.einsum('hqk,qhe->khe', grad_scores, query_blk)
        key_acc = lax.dynamic_update_slice_in_dim(key_acc, lax.dynamic_slice_in_dim(key_acc, offset, span, 0) + grad_key, offset, 0)
        value_acc = lax.dynamic_update_slice_in_dim(value_acc, lax.dynamic_slice_in_dim(value_acc, offset, span, 0) + grad_value, offset, 0)
        return ((key_acc, value_acc), grad_query)
    (key_acc, value_acc), grad_query = lax.scan(one_block, (zero_pad, zero_pad), jnp.arange(length_all // block_rows, dtype=jnp.int32))
    grad_query = grad_query.reshape(length_all, HEADS, HEAD)
    return (grad_query, key_acc[WIN:WIN + length_all], value_acc[WIN:WIN + length_all])

def one_sequence(hidden_in, cotangent, w_qkv, w_out, w_in, w_down, norm_scales):
    length_all = hidden_in.shape[0]
    inner_dim = HEADS * HEAD
    block_rows = math.gcd(512, length_all)
    norm_gains = norm_scales.astype(jnp.float32)
    inputs_f = hidden_in.astype(jnp.float32)
    normed_one, inv_one, scaled_one = layer_norm(inputs_f, norm_gains[0])
    norm_in = rounded(scaled_one)
    projected = jnp.dot(norm_in, w_qkv, preferred_element_type=jnp.float32)
    cosine_tab, sine_tab = rope_tables(jnp.arange(length_all, dtype=jnp.int32))
    query_raw = projected[:, :inner_dim].reshape(length_all, HEADS, HEAD)
    key_raw = projected[:, inner_dim:2 * inner_dim].reshape(length_all, HEADS, HEAD)
    query_rot = rounded(query_raw * cosine_tab + rotate_half(query_raw) * sine_tab)
    key_rot = rounded(key_raw * cosine_tab + rotate_half(key_raw) * sine_tab)
    value_b = rounded(projected[:, 2 * inner_dim:].reshape(length_all, HEADS, HEAD))
    context, log_total = attend_forward(query_rot, key_rot, value_b, block_rows)
    residual = inputs_f + jnp.dot(context, w_out, preferred_element_type=jnp.float32)
    normed_two, inv_two, scaled_two = layer_norm(residual, norm_gains[1])
    norm_ffn = rounded(scaled_two)
    ffn_in = jnp.dot(norm_ffn, w_in, preferred_element_type=jnp.float32)
    act_in = ffn_in[:, :FF]
    gate_in = ffn_in[:, FF:]
    gelu_act, gelu_slope = gelu_parts(act_in)
    hidden_act = rounded(gelu_act * gate_in)
    output_f = residual + jnp.dot(hidden_act, w_down, preferred_element_type=jnp.float32)
    grad_hidden = jnp.dot(cotangent, w_down.T, preferred_element_type=jnp.float32)
    grad_ffn_in = rounded(jnp.concatenate([grad_hidden * gate_in * gelu_slope, grad_hidden * gelu_act], axis=1))
    back_two = jnp.dot(grad_ffn_in, w_in.T, preferred_element_type=jnp.float32)
    residual_grad = cotangent.astype(jnp.float32) + norm_back(back_two, normed_two, inv_two, norm_gains[1])
    residual_b = rounded(residual_grad)
    grad_context = rounded(jnp.dot(residual_b, w_out.T, preferred_element_type=jnp.float32))
    grad_query, grad_key, grad_value = attend_backward(query_rot, key_rot, value_b, context, log_total, grad_context, block_rows)
    grad_query = grad_query * cosine_tab - rotate_half(grad_query) * sine_tab
    grad_key = grad_key * cosine_tab - rotate_half(grad_key) * sine_tab
    grad_proj = rounded(jnp.concatenate([grad_query.reshape(length_all, inner_dim), grad_key.reshape(length_all, inner_dim), grad_value.reshape(length_all, inner_dim)], axis=1))
    back_one = jnp.dot(grad_proj, w_qkv.T, preferred_element_type=jnp.float32)
    input_grad = residual_grad + norm_back(back_one, normed_one, inv_one, norm_gains[0])
    scale_grads = jnp.stack([lax.optimization_barrier(jnp.sum(back_one * normed_one, axis=0)), lax.optimization_barrier(jnp.sum(back_two * normed_two, axis=0))])
    weight_grads = (jnp.dot(norm_in.T, grad_proj, preferred_element_type=jnp.float32), jnp.dot(context.T, residual_b, preferred_element_type=jnp.float32), jnp.dot(norm_ffn.T, grad_ffn_in, preferred_element_type=jnp.float32), jnp.dot(hidden_act.T, cotangent, preferred_element_type=jnp.float32), scale_grads)
    return (output_f.astype(jnp.bfloat16), input_grad, weight_grads)

def reference(hidden_in, w_qkv, w_out, w_in, w_down, norm_scales, cotangent):

    def per_sequence(running, seq_pair):
        layer_rows, input_grad, weight_grads = one_sequence(seq_pair[0], seq_pair[1], w_qkv, w_out, w_in, w_down, norm_scales)
        return (tuple((summed + added for summed, added in zip(running, weight_grads))), (layer_rows, input_grad))
    zeros_init = (jnp.zeros(w_qkv.shape, jnp.float32), jnp.zeros(w_out.shape, jnp.float32), jnp.zeros(w_in.shape, jnp.float32), jnp.zeros(w_down.shape, jnp.float32), jnp.zeros(norm_scales.shape, jnp.float32))
    totals, (layer_out, grad_input) = lax.scan(per_sequence, zeros_init, (hidden_in, cotangent))
    return (layer_out, grad_input, totals[0], totals[1], totals[2], totals[3], totals[4])
```

```python
import math

import jax
import jax.numpy as jnp
from jax import lax
from jax.sharding import PartitionSpec as P

HEADS = 8
HEAD = 64
FF = 1312
WIN = 64


norm_eps = 1e-05
rope_theta = 10000.0


def swap(values, axis_name, mask):
    count = lax.axis_size(axis_name)
    return lax.ppermute(values, axis_name, [(i, i ^ mask) for i in range(count)])


def after(values, *earlier):
    return lax.optimization_barrier((values,) + earlier)[0]


def edge_exchange(last_rows, first_rows, axis):
    count = lax.axis_size(axis)
    forward = [(i, i + 1) for i in range(count - 1)]
    backward = [(target, source) for source, target in forward]
    return lax.ppermute(last_rows, axis, forward), lax.ppermute(first_rows, axis, backward)


def relative(values, axis):
    own = lax.axis_index("fsdp")
    count = lax.axis_size("fsdp")
    width = values.shape[axis] // count
    step = 1
    while step < count:
        parts = [lax.slice_in_dim(values, k * width, (k + 1) * width, axis=axis) for k in range(count)]
        swapped = jnp.concatenate([parts[k ^ step] for k in range(count)], axis=axis)
        values = jnp.where((own & step) != 0, swapped, values)
        step *= 2
    return values


def gather_blocks(shard, axis, earlier):
    shard = after(shard, *earlier)
    far = swap(shard, "fsdp", 2)
    near = swap(shard, "fsdp", 1)
    relay = swap(far, "fsdp", 1)
    return jnp.concatenate([shard, near, far, relay], axis=axis), far


def seq_stages():
    bits = []
    step = 1
    count = lax.axis_size("seq")
    while step < count:
        bits.append(step)
        step *= 2
    stages = [[b] for b in bits[:1]]
    rest = bits[1:]
    while rest:
        stages.append(rest[:2])
        rest = rest[2:]
    return stages


def masks_of(stage):
    masks = [0]
    for b in stage:
        masks = masks + [m | b for m in masks]
    return masks


def sum_over_seq(total, axis):
    own = lax.axis_index("seq")
    stages = seq_stages()
    for stage in stages:
        masks = masks_of(stage)
        base = stage[0]
        place = own // base % len(masks)
        width = total.shape[axis] // len(masks)
        piece = lambda m: lax.dynamic_slice_in_dim(total, (place ^ (m // base)) * width, width, axis=axis)
        got = [swap(piece(m).astype(jnp.bfloat16), "seq", m) for m in masks[1:]]
        kept = piece(0)
        for g in got:
            kept = kept + g.astype(jnp.float32)
        total = kept
    done = total.astype(jnp.bfloat16)
    order = [0]
    for stage in reversed(stages):
        masks = masks_of(stage)
        got = [done] + [swap(done, "seq", m) for m in masks[1:]]
        done = jnp.concatenate(got, axis=axis)
        order = [m ^ o for m in masks for o in order]
    count = len(order)
    width = done.shape[axis] // count
    where_is = {m: k for k, m in enumerate(order)}
    slots = []
    for stage in stages:
        slots = [s | m for s in (slots or [0]) for m in masks_of(stage)]
    slot_of = jnp.array([where_is[m] for m in range(count)], jnp.int32)
    parts = [
        lax.dynamic_slice_in_dim(done, slot_of[own ^ s] * width, width, axis=axis) for s in slots
    ]
    return jnp.concatenate(parts, axis=axis).astype(jnp.float32)


def reduce_blocks(kept, sent):
    got = swap(jnp.stack(sent).astype(jnp.bfloat16), "fsdp", 1)
    far = swap((kept[1] + got[1].astype(jnp.float32)).astype(jnp.bfloat16), "fsdp", 2)
    return kept[0] + got[0].astype(jnp.float32) + far.astype(jnp.float32)


def block(values, j, axis):
    width = values.shape[axis] // lax.axis_size("fsdp")
    return lax.slice_in_dim(values, j * width, (j + 1) * width, axis=axis)


def pair(values, j, axis):
    return jnp.concatenate([block(values, j, axis), block(values, j + 2, axis)], axis=axis)


def weight_grad(left, right, axis):
    halves = []
    for j in (0, 1):
        if axis == 0:
            both = inner_rows(pair(left, j, 1), right)
        else:
            both = inner_rows(left, pair(right, j, 1))
        width = both.shape[axis] // 2
        halves.append(
            [lax.slice_in_dim(both, k * width, (k + 1) * width, axis=axis) for k in (0, 1)]
        )
    return reduce_blocks(halves[0], halves[1])


def rounded(values):
    return lax.optimization_barrier(values.astype(jnp.bfloat16))


def layer_norm(residual, gain_vec):
    average = jnp.mean(residual, axis=-1, keepdims=True)
    centred = residual - average
    variance = jnp.mean(centred * centred, axis=-1, keepdims=True)
    inv_std = lax.rsqrt(variance + norm_eps)
    normed = centred * inv_std
    return (normed, inv_std, normed * gain_vec)


def norm_back(upstream, normed, inv_std, gain_vec):
    through = upstream * gain_vec
    first_mean = jnp.mean(through, axis=-1, keepdims=True)
    second_mean = jnp.mean(through * normed, axis=-1, keepdims=True)
    return inv_std * (through - first_mean - normed * second_mean)


def rope_tables(positions):
    half_dim = HEAD // 2
    frequency = jnp.exp(
        jnp.arange(half_dim, dtype=jnp.float32) * (-2.0 * math.log(rope_theta) / HEAD)
    )
    angles = positions.astype(jnp.float32)[:, None] * frequency[None, :]
    angles = jnp.concatenate([angles, angles], axis=1)
    return (jnp.cos(angles)[:, None, :], jnp.sin(angles)[:, None, :])


def rotate_half(values):
    half_dim = values.shape[-1] // 2
    return jnp.concatenate([-values[..., half_dim:], values[..., :half_dim]], axis=-1)


def band_mask(offset, query_count, key_count, length_all):
    query_pos = offset + jnp.arange(query_count, dtype=jnp.int32)[:, None]
    key_pos = offset - WIN + jnp.arange(key_count, dtype=jnp.int32)[None, :]
    in_window = jnp.abs(query_pos - key_pos) <= WIN
    return in_window & (key_pos >= 0) & (key_pos < length_all)


def gelu_parts(act_in):
    cumulative = 0.5 * (1.0 + lax.erf(act_in * (1.0 / math.sqrt(2.0))))
    density = jnp.exp(-0.5 * act_in * act_in) * (1.0 / math.sqrt(2.0 * math.pi))
    return (act_in * cumulative, cumulative + act_in * density)


def inner_rows(left, right):
    return lax.dot_general(
        left, right, (((0,), (0,)), ((), ())), preferred_element_type=jnp.float32
    )


def times_transposed(left, right):
    return lax.dot_general(
        left, right, (((1,), (1,)), ((), ())), preferred_element_type=jnp.float32
    )


def per_device(hidden_in, w_qkv, w_out, w_in, w_down, norm_scales, cotangent):
    full_qkv, far_qkv = gather_blocks(w_qkv, 0, ())
    full_out, far_out = gather_blocks(w_out, 0, (far_qkv,))
    full_in_t, far_in = gather_blocks(w_in.T, 1, (far_out,))
    full_down, _ = gather_blocks(w_down, 0, (far_in,))
    near_scales = swap(norm_scales, "fsdp", 1)
    both_scales = jnp.concatenate([norm_scales, near_scales], axis=1)
    norm_gains = relative(
        jnp.concatenate([both_scales, swap(both_scales, "fsdp", 2)], axis=1), 1
    )
    inputs_b = hidden_in[0]
    upstream_b = cotangent[0]
    local_len = inputs_b.shape[0]
    inner_dim = HEADS * HEAD
    ext_len = local_len + 2 * WIN
    offset = lax.axis_index("seq") * local_len
    length_all = lax.axis_size("seq") * local_len
    score_scale = 1.0 / math.sqrt(HEAD)
    inputs_f = inputs_b.astype(jnp.float32)
    normed_one, inv_one, scaled_one = layer_norm(inputs_f, norm_gains[0])
    norm_in = rounded(relative(scaled_one, 1))
    projected = jnp.dot(norm_in, full_qkv, preferred_element_type=jnp.float32)
    cosine_tab, sine_tab = rope_tables(offset + jnp.arange(local_len, dtype=jnp.int32))
    query_raw = projected[:, :inner_dim].reshape(local_len, HEADS, HEAD)
    key_raw = projected[:, inner_dim : 2 * inner_dim].reshape(local_len, HEADS, HEAD)
    query_rot = rounded(query_raw * cosine_tab + rotate_half(query_raw) * sine_tab)
    key_rot = rounded(key_raw * cosine_tab + rotate_half(key_raw) * sine_tab)
    value_b = rounded(projected[:, 2 * inner_dim :])
    key_value = jnp.concatenate([key_rot.reshape(local_len, inner_dim), value_b], axis=1)
    low, high = edge_exchange(key_value[local_len - WIN :], key_value[:WIN], "seq")
    extended = jnp.concatenate([low, key_value, high], axis=0)
    key_ext = extended[:, :inner_dim].reshape(ext_len, HEADS, HEAD)
    value_ext = extended[:, inner_dim:].reshape(ext_len, HEADS, HEAD)
    allowed = band_mask(offset, local_len, ext_len, length_all)[None]

    def masked_scores():
        scores = (
            jnp.einsum("qhe,khe->hqk", query_rot, key_ext, preferred_element_type=jnp.float32)
            * score_scale
        )
        return jnp.where(allowed, scores, -jnp.inf)

    scores = masked_scores()
    top_score = jnp.max(scores, axis=-1, keepdims=True)
    totals = jnp.sum(jnp.exp(scores - top_score), axis=-1, keepdims=True)
    log_total = top_score + jnp.log(totals)
    probs_b = rounded(jnp.exp(scores - log_total))
    context_heads = rounded(
        jnp.einsum("hqk,khe->qhe", probs_b, value_ext, preferred_element_type=jnp.float32)
    )
    context = relative(context_heads.reshape(local_len, inner_dim), 1)
    residual = inputs_f + jnp.dot(context, full_out, preferred_element_type=jnp.float32)
    normed_two, inv_two, scaled_two = layer_norm(residual, norm_gains[1])
    norm_ffn = rounded(relative(scaled_two, 1))
    ffn_t = times_transposed(full_in_t, norm_ffn)
    half = ffn_t.shape[0] // 2
    act_t = ffn_t[:half]
    gate_t = ffn_t[half:]
    gelu_act, gelu_slope = gelu_parts(act_t)
    hidden_t = rounded(relative(gelu_act * gate_t, 0))
    layer_out = (residual + inner_rows(hidden_t, full_down)).astype(jnp.bfloat16)
    down_parts = [
        [jnp.dot(block(hidden_t, j, 0), upstream_b, preferred_element_type=jnp.float32) for j in js]
        for js in ((0, 2), (1, 3))
    ]
    share_down = reduce_blocks(*down_parts)
    grad_hidden = relative(times_transposed(full_down, upstream_b), 0)
    grad_ffn_t = rounded(
        jnp.concatenate([grad_hidden * gate_t * gelu_slope, grad_hidden * gelu_act], axis=0)
    )
    back_two = relative(inner_rows(grad_ffn_t, full_in_t), 1)
    in_parts = []
    for j in (0, 1):
        both = jnp.dot(grad_ffn_t, pair(norm_ffn, j, 1), preferred_element_type=jnp.float32)
        width = both.shape[1] // 2
        in_parts.append([both[:, :width], both[:, width:]])
    share_in_t = reduce_blocks(*in_parts)
    residual_grad = upstream_b.astype(jnp.float32) + norm_back(
        back_two, normed_two, inv_two, norm_gains[1]
    )
    residual_b = rounded(residual_grad)
    share_out = weight_grad(context, residual_b, 0)
    grad_heads = rounded(relative(times_transposed(residual_b, full_out), 1)).reshape(
        local_len, HEADS, HEAD
    )
    delta_all = jnp.sum(grad_heads.astype(jnp.float32) * context_heads.astype(jnp.float32), axis=-1)
    scores = masked_scores()
    probs_f = jnp.exp(scores - log_total)
    probs_b = rounded(probs_f)
    grad_value = jnp.einsum("hqk,qhe->khe", probs_b, grad_heads, preferred_element_type=jnp.float32)
    grad_probs = jnp.einsum(
        "qhe,khe->hqk", grad_heads, value_ext, preferred_element_type=jnp.float32
    )
    grad_scores = rounded(probs_f * (grad_probs - delta_all.T[:, :, None]) * score_scale)
    grad_query = jnp.einsum(
        "hqk,khe->qhe", grad_scores, key_ext, preferred_element_type=jnp.float32
    )
    grad_key = jnp.einsum(
        "hqk,qhe->khe", grad_scores, query_rot, preferred_element_type=jnp.float32
    )
    key_value_grad = jnp.concatenate(
        [grad_key.reshape(ext_len, inner_dim), grad_value.reshape(ext_len, inner_dim)], axis=1
    )
    low, high = edge_exchange(
        key_value_grad[WIN + local_len :].astype(jnp.bfloat16),
        key_value_grad[:WIN].astype(jnp.bfloat16),
        "seq",
    )
    own_rows = key_value_grad[WIN : WIN + local_len]
    own_rows = jnp.concatenate(
        [
            own_rows[:WIN] + low.astype(jnp.float32),
            own_rows[WIN : local_len - WIN],
            own_rows[local_len - WIN :] + high.astype(jnp.float32),
        ],
        axis=0,
    )
    grad_key_own = own_rows[:, :inner_dim].reshape(local_len, HEADS, HEAD)
    grad_query = grad_query * cosine_tab - rotate_half(grad_query) * sine_tab
    grad_key_own = grad_key_own * cosine_tab - rotate_half(grad_key_own) * sine_tab
    grad_proj = rounded(
        jnp.concatenate(
            [
                grad_query.reshape(local_len, inner_dim),
                grad_key_own.reshape(local_len, inner_dim),
                own_rows[:, inner_dim:],
            ],
            axis=1,
        )
    )
    share_qkv = weight_grad(norm_in, grad_proj, 0)
    back_one = relative(times_transposed(grad_proj, full_qkv), 1)
    input_grad = residual_grad + norm_back(back_one, normed_one, inv_one, norm_gains[0])
    scale_grads = relative(
        jnp.stack([jnp.sum(back_one * normed_one, axis=0), jnp.sum(back_two * normed_two, axis=0)]),
        1,
    )
    near = swap(pair(scale_grads, 1, 1), "fsdp", 1) + pair(scale_grads, 0, 1)
    width = near.shape[1] // 2
    share_scales = near[:, :width] + swap(near[:, width:], "fsdp", 2)
    for stage in seq_stages():
        got = [swap(share_scales, "seq", m) for m in masks_of(stage)[1:]]
        for g in got:
            share_scales = share_scales + g
    return (
        layer_out[None],
        input_grad[None],
        sum_over_seq(share_qkv, 0),
        sum_over_seq(share_out, 0),
        sum_over_seq(share_in_t, 0).T,
        sum_over_seq(share_down, 1),
        share_scales,
    )


def solution(mesh):
    placed = (
        P("fsdp", "seq", None),
        P("fsdp", None),
        P("fsdp", None),
        P("fsdp", None),
        P("fsdp", None),
        P(None, "fsdp"),
        P("fsdp", "seq", None),
    )
    return jax.shard_map(
        per_device,
        mesh=mesh,
        in_specs=placed,
        out_specs=(
            P("fsdp", "seq", None),
            P("fsdp", "seq", None),
            P("fsdp", None),
            P("fsdp", None),
            P("fsdp", None),
            P("fsdp", None),
            P(None, "fsdp"),
        ),
        check_vma=False,
    )
```

```python
import math

import jax
import jax.numpy as jnp
from jax import lax
from jax.sharding import PartitionSpec as P

HEADS = 8
HEAD = 64
FF = 1312
WIN = 64


norm_eps = 1e-05
rope_theta = 10000.0


def swap(values, axis_name, mask):
    count = lax.axis_size(axis_name)
    return lax.ppermute(values, axis_name, [(i, i ^ mask) for i in range(count)])


def sync(*values):
    return lax.optimization_barrier(values)


def edge_exchange(last_rows, first_rows, axis):
    count = lax.axis_size(axis)
    forward = [(i, i + 1) for i in range(count - 1)]
    backward = [(target, source) for source, target in forward]
    return lax.ppermute(last_rows, axis, forward), lax.ppermute(first_rows, axis, backward)


def own_bit(axis_name, mask):
    return (lax.axis_index(axis_name) // mask) % 2


def half_at(values, which, axis):
    width = values.shape[axis] // 2
    return lax.dynamic_slice_in_dim(values, which * width, width, axis=axis)


def join_at(mine, other, which, axis):
    return jnp.where(
        which == 0,
        jnp.concatenate([mine, other], axis=axis),
        jnp.concatenate([other, mine], axis=axis),
    )


def relative(values, axis):
    own = lax.axis_index("fsdp")
    count = lax.axis_size("fsdp")
    width = values.shape[axis] // count
    step = 1
    while step < count:
        parts = [lax.slice_in_dim(values, k * width, (k + 1) * width, axis=axis) for k in range(count)]
        swapped = jnp.concatenate([parts[k ^ step] for k in range(count)], axis=axis)
        values = jnp.where((own & step) != 0, swapped, values)
        step *= 2
    return values


def block(values, j, axis):
    width = values.shape[axis] // lax.axis_size("fsdp")
    return lax.slice_in_dim(values, j * width, (j + 1) * width, axis=axis)


def pair(values, j, axis):
    return jnp.concatenate([block(values, j, axis), block(values, j + 2, axis)], axis=axis)


class Shard:
    def __init__(self, own, axis):
        self.own, self.axis = own, axis
        self.which = own_bit("seq", 1)

    def far_half(self):
        return half_at(self.own, self.which, self.axis)

    def stacked(self, near, far, relay):
        index = lax.axis_index("fsdp")
        count = lax.axis_size("fsdp")
        full = jnp.zeros((count,) + self.own.shape, self.own.dtype)
        for j, part in enumerate((self.own, near, far, relay)):
            full = lax.dynamic_update_index_in_dim(full, part, index ^ j, 0)
        return full.reshape((-1,) + self.own.shape[1:])


class Share:
    def __init__(self, kept, sent, axis):
        self.axis = axis
        self.kept, self.sent = kept, sent
        bits = []
        step = 1
        while step < lax.axis_size("seq"):
            bits.append(step)
            step *= 2
        self.todo = [("fsdp", 1, "near"), ("fsdp", 2, "far")]
        self.todo += [("seq", b, "halve") for b in bits]
        self.todo += [("seq", b, "double") for b in reversed(bits)]
        self.total = None

    def send(self):
        axis_name, mask, kind = self.todo[0]
        if kind == "near":
            payload = jnp.stack(self.sent).astype(jnp.bfloat16)
        elif kind == "far":
            payload = self.kept[1].astype(jnp.bfloat16)
        elif kind == "halve":
            which = own_bit(axis_name, mask)
            payload = half_at(self.total, 1 - which, self.axis).astype(jnp.bfloat16)
        else:
            payload = self.total = self.total.astype(jnp.bfloat16)
        return swap(payload, axis_name, mask)

    def take(self, got):
        axis_name, mask, kind = self.todo.pop(0)
        if kind == "near":
            got = got.astype(jnp.float32)
            self.kept = [self.kept[0] + got[0], self.kept[1] + got[1]]
        elif kind == "far":
            self.total = self.kept[0] + got.astype(jnp.float32)
        elif kind == "halve":
            which = own_bit(axis_name, mask)
            self.total = half_at(self.total, which, self.axis) + got.astype(jnp.float32)
        else:
            self.total = join_at(self.total, got, own_bit(axis_name, mask), self.axis)

    def result(self):
        assert not self.todo
        return self.total.astype(jnp.float32)


def advance(shares, *others):
    live = [s for s in shares if s.todo]
    out = sync(*[s.send() for s in live], *others)
    for s, got in zip(live, out):
        s.take(got)
    return out[len(live) :]


def weight_share(left, right, split):
    halves = []
    for j in (0, 1):
        if split == 0:
            both = inner_rows(pair(left, j, 1), right)
        else:
            both = jnp.dot(left, pair(right, j, 1), preferred_element_type=jnp.float32)
        width = both.shape[split] // 2
        halves.append(
            [lax.slice_in_dim(both, k * width, (k + 1) * width, axis=split) for k in (0, 1)]
        )
    return Share(halves[0], halves[1], 0)


def rounded(values):
    return lax.optimization_barrier(values.astype(jnp.bfloat16))


def layer_norm(residual, gain_vec):
    average = jnp.mean(residual, axis=-1, keepdims=True)
    centred = residual - average
    variance = jnp.mean(centred * centred, axis=-1, keepdims=True)
    inv_std = lax.rsqrt(variance + norm_eps)
    normed = centred * inv_std
    return (normed, inv_std, normed * gain_vec)


def norm_back(upstream, normed, inv_std, gain_vec):
    through = upstream * gain_vec
    first_mean = jnp.mean(through, axis=-1, keepdims=True)
    second_mean = jnp.mean(through * normed, axis=-1, keepdims=True)
    return inv_std * (through - first_mean - normed * second_mean)


def rope_tables(positions):
    half_dim = HEAD // 2
    frequency = jnp.exp(
        jnp.arange(half_dim, dtype=jnp.float32) * (-2.0 * math.log(rope_theta) / HEAD)
    )
    angles = positions.astype(jnp.float32)[:, None] * frequency[None, :]
    angles = jnp.concatenate([angles, angles], axis=1)
    return (jnp.cos(angles)[:, None, :], jnp.sin(angles)[:, None, :])


def rotate_half(values):
    half_dim = values.shape[-1] // 2
    return jnp.concatenate([-values[..., half_dim:], values[..., :half_dim]], axis=-1)


def band_mask(offset, query_count, key_count, length_all):
    query_pos = offset + jnp.arange(query_count, dtype=jnp.int32)[:, None]
    key_pos = offset - WIN + jnp.arange(key_count, dtype=jnp.int32)[None, :]
    in_window = jnp.abs(query_pos - key_pos) <= WIN
    return in_window & (key_pos >= 0) & (key_pos < length_all)


def gelu_parts(act_in):
    cumulative = 0.5 * (1.0 + lax.erf(act_in * (1.0 / math.sqrt(2.0))))
    density = jnp.exp(-0.5 * act_in * act_in) * (1.0 / math.sqrt(2.0 * math.pi))
    return (act_in * cumulative, cumulative + act_in * density)


def inner_rows(left, right):
    return lax.dot_general(
        left, right, (((0,), (0,)), ((), ())), preferred_element_type=jnp.float32
    )


def times_transposed(left, right):
    return lax.dot_general(
        left, right, (((1,), (1,)), ((), ())), preferred_element_type=jnp.float32
    )


def per_device(hidden_in, w_qkv, w_out, w_in, w_down, norm_scales, cotangent):
    inputs_b = hidden_in[0]
    upstream_b = cotangent[0]
    local_len = inputs_b.shape[0]
    inner_dim = HEADS * HEAD
    ext_len = local_len + 2 * WIN
    offset = lax.axis_index("seq") * local_len
    length_all = lax.axis_size("seq") * local_len
    score_scale = 1.0 / math.sqrt(HEAD)
    half = w_in.shape[1] // 2
    seq_bit = own_bit("seq", 1)
    w_in_t = w_in.T
    s_qkv = Shard(w_qkv, 0)
    s_out = Shard(w_out, 0)
    s_act = Shard(w_in_t[:half], 0)
    s_gate = Shard(w_in_t[half:], 0)
    s_down = Shard(w_down, 1)

    qkv_mine = swap(s_qkv.far_half(), "fsdp", 2)
    qkv_near = swap(s_qkv.own, "fsdp", 1)
    scales_near = swap(norm_scales, "fsdp", 1)
    inputs_f = inputs_b.astype(jnp.float32)
    average = jnp.mean(inputs_f, axis=-1, keepdims=True)
    centred = inputs_f - average
    inv_one = lax.rsqrt(jnp.mean(centred * centred, axis=-1, keepdims=True) + norm_eps)
    normed_one = centred * inv_one
    cosine_tab, sine_tab = rope_tables(offset + jnp.arange(local_len, dtype=jnp.int32))
    qkv_mine, qkv_near, scales_near, own_out, own_act, own_gate, own_down = sync(
        qkv_mine, qkv_near, scales_near, s_out.own, s_act.own, s_gate.own, s_down.own
    )
    s_out.own, s_act.own, s_gate.own, s_down.own = own_out, own_act, own_gate, own_down

    qkv_other = swap(qkv_mine, "seq", 1)
    both_scales = jnp.concatenate([norm_scales, scales_near], axis=1)
    scales_far = swap(both_scales, "fsdp", 2)
    out_mine = swap(s_out.far_half(), "fsdp", 2)
    act_mine = swap(s_act.far_half(), "fsdp", 2)
    out_near = swap(s_out.own, "fsdp", 1)
    act_near = swap(s_act.own, "fsdp", 1)
    qkv_other, scales_far, out_mine, act_mine, out_near, act_near, own_gate, own_down = sync(
        qkv_other, scales_far, out_mine, act_mine, out_near, act_near, s_gate.own, s_down.own
    )
    s_gate.own, s_down.own = own_gate, own_down

    qkv_far = join_at(qkv_mine, qkv_other, seq_bit, 0)
    qkv_relay = swap(qkv_far, "fsdp", 1)
    gate_mine = swap(s_gate.far_half(), "fsdp", 2)
    out_other = swap(out_mine, "seq", 1)
    act_other = swap(act_mine, "seq", 1)
    gate_near = swap(s_gate.own, "fsdp", 1)
    norm_gains = relative(jnp.concatenate([both_scales, scales_far], axis=1), 1)
    norm_in = rounded(normed_one * norm_gains[0])
    full_qkv = s_qkv.stacked(qkv_near, qkv_far, qkv_relay)
    projected = jnp.dot(norm_in, full_qkv, preferred_element_type=jnp.float32)
    query_raw = projected[:, :inner_dim].reshape(local_len, HEADS, HEAD)
    key_raw = projected[:, inner_dim : 2 * inner_dim].reshape(local_len, HEADS, HEAD)
    query_rot = rounded(query_raw * cosine_tab + rotate_half(query_raw) * sine_tab)
    key_rot = rounded(key_raw * cosine_tab + rotate_half(key_raw) * sine_tab)
    value_b = rounded(projected[:, 2 * inner_dim :])
    key_value = jnp.concatenate([key_rot.reshape(local_len, inner_dim), value_b], axis=1)
    low, high = edge_exchange(key_value[local_len - WIN :], key_value[:WIN], "seq")
    out_other, act_other, gate_mine, gate_near, low, high, key_value, own_down = sync(
        out_other, act_other, gate_mine, gate_near, low, high, key_value, s_down.own
    )
    s_down.own = own_down

    down_mine = swap(s_down.far_half(), "fsdp", 2)
    gate_other = swap(gate_mine, "seq", 1)
    out_far = join_at(out_mine, out_other, seq_bit, 0)
    act_far = join_at(act_mine, act_other, seq_bit, 0)
    out_relay = swap(out_far, "fsdp", 1)
    act_relay = swap(act_far, "fsdp", 1)
    down_near = swap(s_down.own, "fsdp", 1)
    extended = jnp.concatenate([low, key_value, high], axis=0)
    key_ext = extended[:, :inner_dim].reshape(ext_len, HEADS, HEAD)
    value_ext = extended[:, inner_dim:].reshape(ext_len, HEADS, HEAD)
    allowed = band_mask(offset, local_len, ext_len, length_all)[None]

    def masked_scores():
        scores = (
            jnp.einsum("qhe,khe->hqk", query_rot, key_ext, preferred_element_type=jnp.float32)
            * score_scale
        )
        return jnp.where(allowed, scores, -jnp.inf)

    scores = masked_scores()
    top_score = jnp.max(scores, axis=-1, keepdims=True)
    totals = jnp.sum(jnp.exp(scores - top_score), axis=-1, keepdims=True)
    log_total = top_score + jnp.log(totals)
    probs_b = rounded(jnp.exp(scores - log_total))
    context_heads = rounded(
        jnp.einsum("hqk,khe->qhe", probs_b, value_ext, preferred_element_type=jnp.float32)
    )
    context = context_heads.reshape(local_len, inner_dim)
    full_out = s_out.stacked(out_near, out_far, out_relay)
    residual = inputs_f + jnp.dot(context, full_out, preferred_element_type=jnp.float32)
    normed_two, inv_two, scaled_two = layer_norm(residual, norm_gains[1])
    norm_ffn = rounded(relative(scaled_two, 1))
    down_mine, gate_other, act_relay, down_near, norm_ffn = sync(
        down_mine, gate_other, act_relay, down_near, norm_ffn
    )

    down_other = swap(down_mine, "seq", 1)
    gate_far = join_at(gate_mine, gate_other, seq_bit, 0)
    gate_relay = swap(gate_far, "fsdp", 1)
    full_act = jnp.concatenate([s_act.own, act_near, act_far, act_relay], axis=1)
    full_gate = jnp.concatenate([s_gate.own, gate_near, gate_far, gate_relay], axis=1)
    act_t = times_transposed(full_act, norm_ffn)
    gate_t = times_transposed(full_gate, norm_ffn)
    gelu_act, gelu_slope = gelu_parts(act_t)
    hidden_t = rounded(gelu_act * gate_t)
    index = lax.axis_index("fsdp")
    hidden_blocks = hidden_t.reshape(lax.axis_size("fsdp"), -1, local_len)
    down_parts = [
        [
            jnp.dot(
                lax.dynamic_index_in_dim(hidden_blocks, index ^ j, 0, keepdims=False),
                upstream_b,
                preferred_element_type=jnp.float32,
            )
            for j in js
        ]
        for js in ((0, 2), (1, 3))
    ]
    g_down = Share(down_parts[0], down_parts[1], 1)
    down_other, g_sent0, g_sent1 = sync(down_other, *g_down.sent)
    g_down.sent = [g_sent0, g_sent1]

    down_far = join_at(down_mine, down_other, seq_bit, 1)
    down_relay = swap(down_far, "fsdp", 1)
    (down_relay,) = advance([g_down], down_relay)

    full_down = s_down.stacked(down_near, down_far, down_relay)
    grad_hidden = times_transposed(full_down, upstream_b)
    grad_act = rounded(grad_hidden * gate_t * gelu_slope)
    grad_gate = rounded(grad_hidden * gelu_act)
    grad_ffn_t = jnp.concatenate([grad_act, grad_gate], axis=0)
    unit = 8 * lax.axis_size("seq")
    cut = (half + unit - 1) // unit * unit
    g_act = weight_share(grad_ffn_t[:cut], norm_ffn, 1)
    g_gate = weight_share(grad_ffn_t[cut:], norm_ffn, 1)
    back_two = relative(inner_rows(grad_act, full_act) + inner_rows(grad_gate, full_gate), 1)
    residual_grad = upstream_b.astype(jnp.float32) + norm_back(
        back_two, normed_two, inv_two, norm_gains[1]
    )
    residual_b = rounded(residual_grad)
    (residual_b,) = advance([g_down, g_act, g_gate], residual_b)

    grad_heads = rounded(times_transposed(residual_b, full_out)).reshape(local_len, HEADS, HEAD)
    g_out = weight_share(relative(context, 1), residual_b, 0)
    delta_all = jnp.sum(grad_heads.astype(jnp.float32) * context_heads.astype(jnp.float32), axis=-1)
    scores = masked_scores()
    probs_f = jnp.exp(scores - log_total)
    probs_b = rounded(probs_f)
    grad_value = jnp.einsum("hqk,qhe->khe", probs_b, grad_heads, preferred_element_type=jnp.float32)
    grad_probs = jnp.einsum(
        "qhe,khe->hqk", grad_heads, value_ext, preferred_element_type=jnp.float32
    )
    grad_scores = rounded(probs_f * (grad_probs - delta_all.T[:, :, None]) * score_scale)
    grad_key = jnp.einsum(
        "hqk,qhe->khe", grad_scores, query_rot, preferred_element_type=jnp.float32
    )
    key_value_grad = jnp.concatenate(
        [grad_key.reshape(ext_len, inner_dim), grad_value.reshape(ext_len, inner_dim)], axis=1
    )
    low, high = edge_exchange(
        key_value_grad[WIN + local_len :].astype(jnp.bfloat16),
        key_value_grad[:WIN].astype(jnp.bfloat16),
        "seq",
    )
    grad_query = jnp.einsum(
        "hqk,khe->qhe", grad_scores, key_ext, preferred_element_type=jnp.float32
    )
    grad_query = grad_query * cosine_tab - rotate_half(grad_query) * sine_tab
    grad_query = rounded(grad_query.reshape(local_len, inner_dim))
    low, high, grad_query = advance([g_down, g_act, g_out], low, high, grad_query)

    own_rows = key_value_grad[WIN : WIN + local_len]
    own_rows = jnp.concatenate(
        [
            own_rows[:WIN] + low.astype(jnp.float32),
            own_rows[WIN : local_len - WIN],
            own_rows[local_len - WIN :] + high.astype(jnp.float32),
        ],
        axis=0,
    )
    grad_key_own = own_rows[:, :inner_dim].reshape(local_len, HEADS, HEAD)
    grad_key_own = grad_key_own * cosine_tab - rotate_half(grad_key_own) * sine_tab
    grad_key_value = rounded(
        jnp.concatenate(
            [grad_key_own.reshape(local_len, inner_dim), own_rows[:, inner_dim:]], axis=1
        )
    )
    norm_in_rel = relative(norm_in, 1)
    g_query = weight_share(norm_in_rel, grad_query, 0)
    g_key_value = weight_share(norm_in_rel, grad_key_value, 0)
    back_one = times_transposed(
        jnp.concatenate([grad_query, grad_key_value], axis=1), full_qkv
    )
    scale_grads = relative(
        jnp.stack([jnp.sum(back_one * normed_one, axis=0), jnp.sum(back_two * normed_two, axis=0)]),
        1,
    )
    back_one, scale_grads = advance(
        [g_down, g_act, g_gate, g_query, g_key_value], back_one, scale_grads
    )

    scale_got = swap(pair(scale_grads, 1, 1), "fsdp", 1)
    input_grad = residual_grad + norm_back(back_one, normed_one, inv_one, norm_gains[0])
    (scale_got,) = advance([g_down, g_act, g_gate, g_out, g_query], scale_got)
    near = pair(scale_grads, 0, 1) + scale_got
    width = near.shape[1] // 2

    scale_got = swap(near[:, width:], "fsdp", 2)
    layer_out = (residual + inner_rows(hidden_t, full_down)).astype(jnp.bfloat16)
    shares = [g_down, g_act, g_gate, g_out, g_query, g_key_value]
    (scale_got,) = advance(shares, scale_got)
    share_scales = near[:, :width] + scale_got
    step = 1
    while any(s.todo for s in shares) or step < lax.axis_size("seq"):
        if step < lax.axis_size("seq"):
            (got,) = advance(shares, swap(share_scales, "seq", step))
            share_scales = share_scales + got
            step *= 2
        else:
            advance(shares)
    return (
        layer_out[None],
        input_grad[None],
        jnp.concatenate([g_query.result(), g_key_value.result()], axis=1),
        g_out.result(),
        jnp.concatenate([g_act.result(), g_gate.result()], axis=0).T,
        g_down.result(),
        share_scales,
    )


def solution(mesh):
    placed = (
        P("fsdp", "seq", None),
        P("fsdp", None),
        P("fsdp", None),
        P("fsdp", None),
        P("fsdp", None),
        P(None, "fsdp"),
        P("fsdp", "seq", None),
    )
    return jax.shard_map(
        per_device,
        mesh=mesh,
        in_specs=placed,
        out_specs=(
            P("fsdp", "seq", None),
            P("fsdp", "seq", None),
            P("fsdp", None),
            P("fsdp", None),
            P("fsdp", None),
            P("fsdp", None),
            P(None, "fsdp"),
        ),
        check_vma=False,
    )
```
